256 devices in a mesh: rows: 64 (over z, y, core), cols: 4 (over x).
Axes of the slice: x: 4, y: 4, z: 8, core: 2. Of those that a mesh axis runs over, the one named last changes fastest.
Arguments:
- snapshot: float32 [24576, 8192], P('rows', 'cols'), may hold values from -270 to 270
- test_matrix: float32 [8192, 256], P('cols'), may hold values from -0.0625 to 0.0625
Outputs:
- projected: float32 [8192, 256], P('cols')
- triangle: float32 [256, 256], replicated
The draws below stay inside these ranges and needn't reach their ends.
All inputs are finite; a program needn't handle non-finite values.
Results may differ from the reference program's by a relative error of at most 0.00007.
Values sent between devices are 32-bit elements; how exact they have to be, the bound alone decides.
A program may use at most 64 MiB of HBM per device.

```python
import math
import jax
import jax.numpy as jnp
from jax import lax

SNAPSHOTS = 8192
SKETCH = 256
POINTS_DEV = 384
POINTS = 24576
N_ROWS = 64


def draw_snapshot(key, part):
    base_key = jax.random.fold_in(key, 11)
    key_rows, key_cols, key_main = jax.random.split(base_key, 3)
    total = POINTS_DEV * N_ROWS
    rise_rows = 1.0 + 2.0 * jnp.arange(total, dtype=jnp.float32) / (total - 1)
    row_scale = rise_rows * jnp.exp(jax.random.uniform(key_rows, (total,), jnp.float32, 0.0, math.log(10.0)))
    rise_cols = 1.0 + 2.0 * jnp.arange(SNAPSHOTS, dtype=jnp.float32) / (SNAPSHOTS - 1)
    col_scale = rise_cols * jnp.exp(jax.random.uniform(key_cols, (SNAPSHOTS,), jnp.float32, 0.0, math.log(2.0)))
    values = jnp.clip(jax.random.normal(key_main, (total, SNAPSHOTS), jnp.float32), -6.0, 6.0)
    return (values * row_scale[:, None] * col_scale[None, :] * 0.25).astype(jnp.float32)


def level_of(own_key, extent, cuts, smallest, top_value):
    loudness, own = 1.0, jax.random.fold_in(own_key, 6)
    for position, blocks in cuts:
        heights = jnp.exp(jax.random.uniform(jax.random.fold_in(own, position), (blocks,), jnp.float32, smallest / len(cuts), top_value / len(cuts)))
        loudness = loudness * jnp.repeat(heights, extent[position] // blocks).reshape([-1 if axis == position else 1 for axis in range(len(extent))])
    return loudness


def bell_draw(key, dims, scale, reach, pieces=(), kind=jnp.bfloat16):
    array = jax.random.normal(key, dims, jnp.float32) * scale
    if len(pieces) > 0:
        array = level_of(key, dims, pieces, -0.22, 0.18) * array
    return jnp.clip(array, min=-reach, max=reach).astype(kind)


def setup_inputs(seed: int = 0) -> dict:
    key_of = jax.random.split(jax.random.key(seed), 3)
    return {
        "snapshot": draw_snapshot(jax.random.fold_in(key_of[2], 71), 0),
        "test_matrix": bell_draw(key_of[1], (SNAPSHOTS, SKETCH), SNAPSHOTS ** -0.5, 0.0625, ((0, 4),), jnp.float32),
    }


def reference(snapshot, test_matrix):
    high = lax.Precision.HIGHEST
    sketch = jnp.dot(snapshot.astype(jnp.float32), test_matrix.astype(jnp.float32), precision=high, preferred_element_type=jnp.float32)
    gram = jnp.dot(sketch.T.astype(jnp.float32), sketch.astype(jnp.float32), precision=high, preferred_element_type=jnp.float32)
    lower = jnp.linalg.cholesky(gram)
    basis_t = jax.scipy.linalg.solve_triangular(lower, sketch.T, lower=True)
    projected = jnp.dot(snapshot.T.astype(jnp.float32), basis_t.T.astype(jnp.float32), precision=high, preferred_element_type=jnp.float32)
    triangle = lower.T / jnp.sqrt(jnp.float32(POINTS))
    return (projected, triangle)
```

```python
import functools

import jax
import jax.numpy as jnp
from jax import lax
from jax.experimental import pallas as pl
from jax.experimental.pallas import tpu as pltpu
from jax.sharding import PartitionSpec as P

HIGH = lax.Precision.HIGHEST
F32 = jnp.float32
BF16 = jnp.bfloat16
MESH = pl.DeviceIdType.MESH
NZ, NY, NX = 8, 4, 4
POINTS, SNAPS, WIDTH = 384, 2048, 256
HALF = WIDTH // 2
SHARE = POINTS // NX
PANEL = 32
TOTAL = 24576


def three_parts(value):
    first = value.astype(BF16)
    rest = value - first.astype(F32)
    second = rest.astype(BF16)
    third = (rest - second.astype(F32)).astype(BF16)
    return first, second, third


def factor_panel(p, g_ref, x_ref):
    top = pl.multiple_of(p * PANEL, PANEL)
    rows = pl.ds(top, PANEL)
    left, right = g_ref[rows, 0:128], g_ref[rows, 128:256]
    own = jnp.where(p < 4, left, right)
    own = pltpu.roll(own, lax.rem(128 - lax.rem(top, 128), 128), 1)
    x_left, x_right = x_ref[rows, 0:128], x_ref[rows, 128:256]
    wide = (left, right, x_left, x_right, own)
    tiles = [[part[8 * g : 8 * g + 8] for part in wide] for g in range(4)]
    sub = lax.broadcasted_iota(jnp.int32, (8, 128), 0)
    for b in range(4):
        column = {}
        for k in range(8):
            for g in range(b, 4):
                lane = tiles[g][4][:, 8 * b + k : 8 * b + k + 1]
                column[g, k] = jnp.broadcast_to(lane, (8, 128))
        for k in range(8):
            scale = lax.rsqrt(jnp.broadcast_to(column[b, k][k : k + 1, :], (8, 128)))
            low = {g: column[g, k] * scale for g in range(b, 4)}
            for m in range(k + 1, 8):
                entry = jnp.broadcast_to(low[b][m : m + 1, :], (8, 128))
                for g in range(b, 4):
                    column[g, m] = column[g, m] - low[g] * entry
            below = jnp.where(sub <= k, 0.0, low[b])
            for w in range(5):
                row = jnp.broadcast_to(tiles[b][w][k : k + 1, :], (8, 128)) * scale
                tiles[b][w] = jnp.where(sub == k, row, tiles[b][w] - below * row)
                for g in range(b + 1, 4):
                    tiles[g][w] = tiles[g][w] - low[g] * row
    for g in range(4):
        lines = pl.ds(top + 8 * g, 8)
        g_ref[lines, 0:128], g_ref[lines, 128:256] = tiles[g][0], tiles[g][1]
        x_ref[lines, 0:128], x_ref[lines, 128:256] = tiles[g][2], tiles[g][3]


def update_below(p, g_ref, x_ref):
    top = pl.multiple_of(p * PANEL, PANEL)
    g, x = g_ref[pl.ds(top, PANEL), :], x_ref[pl.ds(top, PANEL), :]
    lane = lax.broadcasted_iota(jnp.int32, (PANEL, WIDTH), 1)
    a, b, c = three_parts(jnp.where(lane >= top + PANEL, g, 0.0))
    lhs = jnp.concatenate([a, a, b, a, c, b], 0)
    dims = (((0,), (0,)), ((), ()))
    for ref, value in ((g_ref, g), (x_ref, x)):
        a, b, c = three_parts(value)
        rhs = jnp.concatenate([a, b, a, c, a, b], 0)
        ref[...] -= lax.dot_general(lhs, rhs, dims, preferred_element_type=F32)


def kernel(
    a_hbm, t_hbm, z_ref, r_ref, x_ref,
    a_ref, t_ref, at_ref, p_ref, s_ref, rx_ref, zs_ref, zo_ref, rs_ref, ry_ref, zy_ref, rz_ref,
    gf_ref, gs_ref, g1_ref, gy_ref, gz_ref, gm_ref,
    load, xs, xr, xas, xar, ss, sr, ys, yr, zs, zr, zas, zar, yas, yar, sas, sar,
    gss, gsr, gys, gyr, gzs, gzr, gas, gar, gbs, gbr,
):
    row, x = lax.axis_index("rows"), lax.axis_index("cols")
    c, y, z = lax.rem(row, 2), lax.rem(row // 2, NY), row // (2 * NY)

    def at(dz=0, dy=0, dx=0, dc=0):
        zz, yy = lax.rem(z + dz, NZ), lax.rem(y + dy, NY)
        xx, cc = lax.rem(x + dx, NX), lax.rem(c + dc, 2)
        return ((zz * NY + yy) * 2 + cc, xx)

    def remote(src, dst, send, recv, device):
        return pltpu.make_async_remote_copy(
            src_ref=src, dst_ref=dst, send_sem=send, recv_sem=recv, device_id=device, device_id_type=MESH
        )

    def cols(h):
        return pl.ds(h * HALF, HALF)

    flat = [(dx, dy) for dx in range(NX) for dy in range(NY) if dx or dy]

    def load_a(k):
        part = pl.ds(k * 256, 256)
        return pltpu.make_async_copy(a_hbm.at[:, part], a_ref.at[:, part], load.at[0, k])

    def load_t(k):
        part = pl.ds(k * 256, 256)
        return pltpu.make_async_copy(t_hbm.at[part, :], t_ref.at[part, :], load.at[1, k])

    for k in range(8):
        load_a(k).start()
        load_t(k).start()
    barrier = pltpu.get_barrier_semaphore()
    friends = [at(dc=1)] + [at(dz=d) for d in range(1, NZ)] + [at(dx=dx, dy=dy) for dx, dy in flat]
    for friend in friends:
        pl.semaphore_signal(barrier, inc=1, device_id=friend, device_id_type=MESH)

    for k in range(8):
        load_a(k).wait()
        load_t(k).wait()
        part = jnp.dot(
            a_ref[:, k * 256 : k * 256 + 256], t_ref[k * 256 : k * 256 + 256, :],
            precision=HIGH, preferred_element_type=F32,
        )
        for h in range(2):
            piece = part[:, h * HALF : h * HALF + HALF]
            p_ref[h] = piece if k == 0 else p_ref[h] + piece
    pl.semaphore_wait(barrier, len(friends))

    def share(index):
        return pl.ds(pl.multiple_of(index * SHARE, SHARE), SHARE)

    def x_scatter(h, d):
        src = p_ref.at[h, share(lax.rem(x + d, NX))]
        return remote(src, rx_ref.at[h, d - 1], xs.at[h, d - 1], xr.at[h, d - 1], at(dx=d))

    def x_gather(h, d):
        mine = s_ref.at[h, share(x)]
        return remote(mine, mine, xas.at[h, d - 1], xar.at[h, d - 1], at(dx=d))

    for h in range(2):
        for d in (2, 1, 3):
            x_scatter(h, d).start()
    for k in range(8):
        at_ref[k * 256 : k * 256 + 256, :] = a_ref[:, k * 256 : k * 256 + 256].T
    for h in range(2):
        for d in (1, 2, 3):
            x_scatter(h, d).wait_recv()
        s_ref[h, share(x), :] = (p_ref[h, share(x), :] + rx_ref[h, 0]) + (rx_ref[h, 1] + rx_ref[h, 2])
        for d in (2, 1, 3):
            x_gather(h, d).start()

    def cross(h, out_ref, core):
        sketch = s_ref[h]

        @pl.loop(0, 4)
        def _(i):
            lines = pl.ds(pl.multiple_of(core * 1024 + i * 256, 256), 256)
            out_ref[h, pl.ds(pl.multiple_of(i * 256, 256), 256), :] = jnp.dot(
                at_ref[lines, :], sketch, precision=HIGH, preferred_element_type=F32
            )

    def s_scatter(h):
        return remote(zs_ref.at[h], rs_ref.at[h], ss.at[h], sr.at[h], at(dc=1))

    def y_scatter(h, d):
        src = zo_ref.at[h, pl.ds(pl.multiple_of(lax.rem(y + d, NY) * 256, 256), 256)]
        return remote(src, ry_ref.at[h, d - 1], ys.at[h, d - 1], yr.at[h, d - 1], at(dy=d))

    def z_scatter(h, d):
        src = zy_ref.at[h, pl.ds(pl.multiple_of(lax.rem(z + d, NZ) * 32, 32), 32)]
        return remote(src, rz_ref.at[h, d - 1], zs.at[h, d - 1], zr.at[h, d - 1], at(dz=d))

    base_c = pl.multiple_of(c * 1024, 1024)
    base_y = pl.multiple_of(base_c + y * 256, 256)
    base_z = pl.multiple_of(base_y + z * 32, 32)

    def z_gather(h, d):
        mine = z_ref.at[pl.ds(base_z, 32), cols(h)]
        return remote(mine, mine, zas.at[h, d - 1], zar.at[h, d - 1], at(dz=d))

    def y_gather(h, d):
        mine = z_ref.at[pl.ds(base_y, 256), cols(h)]
        return remote(mine, mine, yas.at[h, d - 1], yar.at[h, d - 1], at(dy=d))

    def s_gather(h):
        mine = z_ref.at[pl.ds(base_c, 1024), cols(h)]
        return remote(mine, mine, sas.at[h], sar.at[h], at(dc=1))

    def to_y(h):
        s_scatter(h).wait_recv()
        zo_ref[h] += rs_ref[h]
        for d in (2, 1, 3):
            y_scatter(h, d).start()

    def to_z(h):
        for d in (1, 2, 3):
            y_scatter(h, d).wait_recv()
        own = zo_ref[h, pl.ds(pl.multiple_of(y * 256, 256), 256), :]
        zy_ref[h] = (own + ry_ref[h, 0]) + (ry_ref[h, 1] + ry_ref[h, 2])
        for d in (4, 3, 5, 2, 6, 1, 7):
            z_scatter(h, d).start()

    def back_z(h):
        for d in range(1, NZ):
            z_scatter(h, d).wait_recv()
        total = zy_ref[h, pl.ds(pl.multiple_of(z * 32, 32), 32), :]
        for d in range(1, NZ):
            total = total + rz_ref[h, d - 1]
        z_ref[pl.ds(base_z, 32), h * HALF : h * HALF + HALF] = total
        for d in (4, 3, 5, 2, 6, 1, 7):
            z_gather(h, d).start()

    def back_y(h):
        for d in range(1, NZ):
            z_gather(h, d).wait_recv()
        for d in (2, 1, 3):
            y_gather(h, d).start()

    def back_s(h):
        for d in (1, 2, 3):
            y_gather(h, d).wait_recv()
        s_gather(h).start()

    def gs_scatter():
        src = gf_ref.at[pl.ds(pl.multiple_of(x * 64 + (1 - c) * 32, 32), 32)]
        return remote(src, gs_ref, gss, gsr, at(dc=1))

    def gy_scatter(d):
        src = g1_ref.at[pl.ds(pl.multiple_of(lax.rem(y + d, NY) * 8, 8), 8)]
        return remote(src, gy_ref.at[d - 1], gys.at[d - 1], gyr.at[d - 1], at(dy=d))

    def gz_all(d):
        mine = gz_ref.at[z]
        return remote(mine, mine, gzs.at[d - 1], gzr.at[d - 1], at(dz=d))

    lines_y = pl.ds(pl.multiple_of(y * 8, 8), 8)

    def g_gather(i):
        mine = gm_ref.at[x, c, lines_y]
        return remote(mine, mine, gas.at[i], gar.at[i], at(dx=flat[i][0], dy=flat[i][1]))

    def gb_gather():
        mine = gm_ref.at[:, c]
        return remote(mine, mine, gbs, gbr, at(dc=1))

    for d in (1, 2, 3):
        x_gather(0, d).wait_recv()
    cross(0, zs_ref, 1 - c)
    s_scatter(0).start()
    cross(0, zo_ref, c)
    for d in (1, 2, 3):
        x_gather(1, d).wait_recv()
    whole = jnp.concatenate([s_ref[0], s_ref[1]], 1)
    gf_ref[...] = lax.dot_general(
        whole, whole, (((0,), (0,)), ((), ())), precision=HIGH, preferred_element_type=F32
    )
    gs_scatter().start()
    cross(1, zs_ref, 1 - c)
    s_scatter(1).start()
    gs_scatter().wait_recv()
    g1_ref[...] = gf_ref[pl.ds(pl.multiple_of(x * 64 + c * 32, 32), 32), :] + gs_ref[...]
    for d in (2, 1, 3):
        gy_scatter(d).start()
    to_y(0)
    cross(1, zo_ref, c)
    for d in (1, 2, 3):
        gy_scatter(d).wait_recv()
    gz_ref[z] = (g1_ref[lines_y, :] + gy_ref[0]) + (gy_ref[1] + gy_ref[2])
    for d in (4, 3, 5, 2, 6, 1, 7):
        gz_all(d).start()
    to_y(1)
    for d in range(1, NZ):
        gz_all(d).wait_recv()
    total = gz_ref[0]
    for i in range(1, NZ):
        total = total + gz_ref[i]
    gm_ref[x, c, lines_y, :] = total
    for i in range(len(flat)):
        g_gather(i).start()
    to_z(0)
    for i in range(len(flat)):
        g_gather(i).wait_recv()
    gb_gather().start()
    x_ref[...] = jnp.where(
        lax.broadcasted_iota(jnp.int32, (WIDTH, WIDTH), 0) == lax.broadcasted_iota(jnp.int32, (WIDTH, WIDTH), 1),
        1.0, 0.0,
    )
    gb_gather().wait_recv()
    r_ref[...] = gm_ref[...].reshape(WIDTH, WIDTH)

    hooks = {0: (to_z, 1), 1: (back_z, 0), 2: (back_z, 1), 3: (back_y, 0), 4: (back_y, 1), 6: (back_s, 0)}

    @pl.loop(0, WIDTH // PANEL)
    def _(p):
        for when, (step, h) in hooks.items():
            pl.when(p == when)(functools.partial(step, h))
        factor_panel(p, r_ref, x_ref)
        update_below(p, r_ref, x_ref)

    line = lax.broadcasted_iota(jnp.int32, (WIDTH, WIDTH), 0)
    lane = lax.broadcasted_iota(jnp.int32, (WIDTH, WIDTH), 1)
    r_ref[...] = jnp.where(lane >= line, r_ref[...], 0.0)
    back_s(1)

    gs_scatter().wait_send()
    gb_gather().wait_send()
    for d in (1, 2, 3):
        gy_scatter(d).wait_send()
    for i in range(len(flat)):
        g_gather(i).wait_send()
    for d in range(1, NZ):
        gz_all(d).wait_send()
    for h in range(2):
        for d in (1, 2, 3):
            x_scatter(h, d).wait_send()
            x_gather(h, d).wait_send()
            y_scatter(h, d).wait_send()
            y_gather(h, d).wait_send()
        for d in range(1, NZ):
            z_scatter(h, d).wait_send()
            z_gather(h, d).wait_send()
        s_scatter(h).wait_send()
    for h in range(2):
        s_gather(h).wait()


def body(snapshot, test_matrix):
    dma = pltpu.SemaphoreType.DMA
    hbm = pl.BlockSpec(memory_space=pl.ANY)
    vmem = pl.BlockSpec(memory_space=pltpu.VMEM)
    cross, factor, inverse = pl.pallas_call(
        kernel,
        out_shape=(
            jax.ShapeDtypeStruct((SNAPS, WIDTH), F32),
            jax.ShapeDtypeStruct((WIDTH, WIDTH), F32),
            jax.ShapeDtypeStruct((WIDTH, WIDTH), F32),
        ),
        in_specs=[hbm, hbm],
        out_specs=(vmem, vmem, vmem),
        scratch_shapes=[
            pltpu.VMEM((POINTS, SNAPS), F32),
            pltpu.VMEM((SNAPS, WIDTH), F32),
            pltpu.VMEM((SNAPS, POINTS), F32),
            pltpu.VMEM((2, POINTS, HALF), F32),
            pltpu.VMEM((2, POINTS, HALF), F32),
            pltpu.VMEM((2, 3, SHARE, HALF), F32),
            pltpu.VMEM((2, 1024, HALF), F32),
            pltpu.VMEM((2, 1024, HALF), F32),
            pltpu.VMEM((2, 1024, HALF), F32),
            pltpu.VMEM((2, 3, 256, HALF), F32),
            pltpu.VMEM((2, 256, HALF), F32),
            pltpu.VMEM((2, 7, 32, HALF), F32),
            pltpu.VMEM((WIDTH, WIDTH), F32),
            pltpu.VMEM((32, WIDTH), F32),
            pltpu.VMEM((32, WIDTH), F32),
            pltpu.VMEM((3, 8, WIDTH), F32),
            pltpu.VMEM((8, 8, WIDTH), F32),
            pltpu.VMEM((4, 2, 32, WIDTH), F32),
            dma((2, 8)),
            dma((2, 3)), dma((2, 3)), dma((2, 3)), dma((2, 3)),
            dma((2,)), dma((2,)),
            dma((2, 3)), dma((2, 3)),
            dma((2, 7)), dma((2, 7)), dma((2, 7)), dma((2, 7)),
            dma((2, 3)), dma((2, 3)),
            dma((2,)), dma((2,)),
            dma, dma,
            dma((3,)), dma((3,)),
            dma((7,)), dma((7,)),
            dma((15,)), dma((15,)),
            dma, dma,
        ],
        compiler_params=pltpu.CompilerParams(
            collective_id=0, has_side_effects=True, vmem_limit_bytes=48 * 1024 * 1024
        ),
        name="range_finder",
    )(snapshot, test_matrix)
    projected = lax.dot_general(
        cross, inverse, (((1,), (1,)), ((), ())), precision=HIGH, preferred_element_type=F32
    )
    return projected, factor / jnp.sqrt(jnp.float32(TOTAL))


def solution(mesh):
    return jax.shard_map(
        body,
        mesh=mesh,
        in_specs=(P("rows", "cols"), P("cols", None)),
        out_specs=(P("cols", None), P()),
        check_vma=False,
    )
```

```python
import functools

import jax
import jax.numpy as jnp
from jax import lax
from jax.experimental import pallas as pl
from jax.experimental.pallas import tpu as pltpu
from jax.sharding import PartitionSpec as P

HIGH = lax.Precision.HIGHEST
F32 = jnp.float32
BF16 = jnp.bfloat16
MESH = pl.DeviceIdType.MESH
NZ, NY, NX = 8, 4, 4
POINTS, SNAPS, WIDTH = 384, 2048, 256
HALF = WIDTH // 2
SHARE = POINTS // NX
PANEL = 32
TOTAL = 24576


def three_parts(value):
    first = value.astype(BF16)
    rest = value - first.astype(F32)
    second = rest.astype(BF16)
    third = (rest - second.astype(F32)).astype(BF16)
    return first, second, third


def factor_panel(p, g_ref, x_ref):
    top = pl.multiple_of(p * PANEL, PANEL)
    rows = pl.ds(top, PANEL)
    left, right = g_ref[rows, 0:128], g_ref[rows, 128:256]
    own = jnp.where(p < 4, left, right)
    own = pltpu.roll(own, lax.rem(128 - lax.rem(top, 128), 128), 1)
    x_left, x_right = x_ref[rows, 0:128], x_ref[rows, 128:256]
    wide = (left, right, x_left, x_right, own)
    tiles = [[part[8 * g : 8 * g + 8] for part in wide] for g in range(4)]
    sub = lax.broadcasted_iota(jnp.int32, (8, 128), 0)
    for b in range(4):
        column = {}
        for k in range(8):
            for g in range(b, 4):
                lane = tiles[g][4][:, 8 * b + k : 8 * b + k + 1]
                column[g, k] = jnp.broadcast_to(lane, (8, 128))
        for k in range(8):
            scale = lax.rsqrt(jnp.broadcast_to(column[b, k][k : k + 1, :], (8, 128)))
            low = {g: column[g, k] * scale for g in range(b, 4)}
            for m in range(k + 1, 8):
                entry = jnp.broadcast_to(low[b][m : m + 1, :], (8, 128))
                for g in range(b, 4):
                    column[g, m] = column[g, m] - low[g] * entry
            below = jnp.where(sub <= k, 0.0, low[b])
            for w in range(5):
                row = jnp.broadcast_to(tiles[b][w][k : k + 1, :], (8, 128)) * scale
                tiles[b][w] = jnp.where(sub == k, row, tiles[b][w] - below * row)
                for g in range(b + 1, 4):
                    tiles[g][w] = tiles[g][w] - low[g] * row
    for g in range(4):
        lines = pl.ds(top + 8 * g, 8)
        g_ref[lines, 0:128], g_ref[lines, 128:256] = tiles[g][0], tiles[g][1]
        x_ref[lines, 0:128], x_ref[lines, 128:256] = tiles[g][2], tiles[g][3]


def update_below(p, g_ref, x_ref):
    top = pl.multiple_of(p * PANEL, PANEL)
    g, x = g_ref[pl.ds(top, PANEL), :], x_ref[pl.ds(top, PANEL), :]
    lane = lax.broadcasted_iota(jnp.int32, (PANEL, WIDTH), 1)
    a, b, c = three_parts(jnp.where(lane >= top + PANEL, g, 0.0))
    lhs = jnp.concatenate([a, a, b, a, c, b], 0)
    dims = (((0,), (0,)), ((), ()))
    for ref, value in ((g_ref, g), (x_ref, x)):
        a, b, c = three_parts(value)
        rhs = jnp.concatenate([a, b, a, c, a, b], 0)
        ref[...] -= lax.dot_general(lhs, rhs, dims, preferred_element_type=F32)


class Copies:
    def __init__(self):
        self.open = {}

    def tracked(self, make):
        return lambda *where: Copy(self.open, make, where)

    def drain(self):
        for (make, where), sides in self.open.items():
            copy = make(*where)
            for side in sides:
                getattr(copy, side)()
        self.open = {}


class Copy:
    def __init__(self, open_copies, make, where):
        self.open, self.key, self.copy = open_copies, (make, where), make(*where)

    def start(self):
        self.copy.start()
        self.open[self.key] = ["wait_recv", "wait_send"]

    def wait_recv(self):
        self.copy.wait_recv()
        self.open[self.key].remove("wait_recv")

    def wait_send(self):
        self.copy.wait_send()
        self.open[self.key].remove("wait_send")


def kernel(
    a_hbm, t_hbm, z_ref, r_ref, x_ref,
    a_ref, t_ref, at_ref, p_ref, s_ref, rx_ref, zs_ref, zo_ref, rs_ref, ry_ref, zy_ref, rz_ref,
    gf_ref, gs_ref, g1_ref, gy_ref, gz_ref, gm_ref,
    load, xs, xr, xas, xar, ss, sr, ys, yr, zs, zr, zas, zar, yas, yar, sas, sar,
    gss, gsr, gys, gyr, gzs, gzr, gas, gar, gbs, gbr,
):
    row, x = lax.axis_index("rows"), lax.axis_index("cols")
    c, y, z = lax.rem(row, 2), lax.rem(row // 2, NY), row // (2 * NY)

    def at(dz=0, dy=0, dx=0, dc=0):
        zz, yy = lax.rem(z + dz, NZ), lax.rem(y + dy, NY)
        xx, cc = lax.rem(x + dx, NX), lax.rem(c + dc, 2)
        return ((zz * NY + yy) * 2 + cc, xx)

    def remote(src, dst, send, recv, device):
        return pltpu.make_async_remote_copy(
            src_ref=src, dst_ref=dst, send_sem=send, recv_sem=recv, device_id=device, device_id_type=MESH
        )

    def cols(h):
        return pl.ds(h * HALF, HALF)

    flat = [(dx, dy) for dx in range(NX) for dy in range(NY) if dx or dy]

    copies = Copies()
    tracked = copies.tracked

    def load_a(k):
        part = pl.ds(k * 256, 256)
        return pltpu.make_async_copy(a_hbm.at[:, part], a_ref.at[:, part], load.at[0, k])

    def load_t(k):
        part = pl.ds(k * 256, 256)
        return pltpu.make_async_copy(t_hbm.at[part, :], t_ref.at[part, :], load.at[1, k])

    for k in range(8):
        load_a(k).start()
        load_t(k).start()
    barrier = pltpu.get_barrier_semaphore()
    friends = [at(dc=1)] + [at(dz=d) for d in range(1, NZ)] + [at(dx=dx, dy=dy) for dx, dy in flat]
    for friend in friends:
        pl.semaphore_signal(barrier, inc=1, device_id=friend, device_id_type=MESH)

    def share(index):
        return pl.ds(pl.multiple_of(index * SHARE, SHARE), SHARE)

    @tracked
    def x_scatter(h, d):
        src = p_ref.at[h, share(lax.rem(x + d, NX))]
        return remote(src, rx_ref.at[h, d - 1], xs.at[h, d - 1], xr.at[h, d - 1], at(dx=d))

    for group in ((2, 1), (3, 0)):
        for k in range(8):
            if group[0] == 2:
                load_a(k).wait()
                load_t(k).wait()
            lines = [share(lax.rem(x + d, NX)) for d in group]
            part = jnp.dot(
                jnp.concatenate([a_ref[line, k * 256 : k * 256 + 256] for line in lines], 0),
                t_ref[k * 256 : k * 256 + 256, :],
                precision=HIGH, preferred_element_type=F32,
            )
            for i, line in enumerate(lines):
                for h in range(2):
                    piece = part[i * SHARE : i * SHARE + SHARE, h * HALF : h * HALF + HALF]
                    p_ref[h, line, :] = piece if k == 0 else p_ref[h, line, :] + piece
        if group[0] == 2:
            pl.semaphore_wait(barrier, len(friends))
        for h in range(2):
            for d in group:
                if d:
                    x_scatter(h, d).start()

    @tracked
    def x_gather(h, d):
        mine = s_ref.at[h, share(x)]
        return remote(mine, mine, xas.at[h, d - 1], xar.at[h, d - 1], at(dx=d))

    for k in range(8):
        at_ref[k * 256 : k * 256 + 256, :] = a_ref[:, k * 256 : k * 256 + 256].T
    for h in range(2):
        for d in (1, 2, 3):
            x_scatter(h, d).wait_recv()
        s_ref[h, share(x), :] = (p_ref[h, share(x), :] + rx_ref[h, 0]) + (rx_ref[h, 1] + rx_ref[h, 2])
        for d in (2, 1, 3):
            x_gather(h, d).start()

    def cross(h, out_ref, core):
        sketch = s_ref[h]

        @pl.loop(0, 4)
        def _(i):
            lines = pl.ds(pl.multiple_of(core * 1024 + i * 256, 256), 256)
            out_ref[h, pl.ds(pl.multiple_of(i * 256, 256), 256), :] = jnp.dot(
                at_ref[lines, :], sketch, precision=HIGH, preferred_element_type=F32
            )

    @tracked
    def s_scatter(h):
        return remote(zs_ref.at[h], rs_ref.at[h], ss.at[h], sr.at[h], at(dc=1))

    pair, bit = z // 2, lax.rem(z, 2)
    FAR = (2, 1, 3, 0)

    def further(s, t):
        return 2 * lax.rem(pair + s, 4) + lax.rem(bit + t, 2)

    def block(index, size):
        return pl.ds(pl.multiple_of(index * size, size), size)

    def others(s):
        return (1,) if s == 0 else (0, 1)

    @tracked
    def y_scatter(h, s, d):
        part = lax.rem(pair + s, 4)
        src = zo_ref.at[h, block(lax.rem(y + d, NY) * 4 + part, 64)]
        return remote(src, ry_ref.at[h, d - 1, block(part, 64)], ys.at[h, s, d - 1], yr.at[h, s, d - 1], at(dy=d))

    @tracked
    def z_scatter(h, s, t):
        src = zy_ref.at[h, block(further(s, t), 32)]
        i = 2 * s + t - 1
        return remote(src, rz_ref.at[h, i], zs.at[h, i], zr.at[h, i], at(dz=further(s, t) - z + NZ))

    @tracked
    def z_gather(h, s, t):
        mine = z_ref.at[c, y, block(z, 32), cols(h)]
        i = 2 * s + t - 1
        return remote(mine, mine, zas.at[h, i], zar.at[h, i], at(dz=further(s, t) - z + NZ))

    @tracked
    def y_gather(h, s, d):
        mine = z_ref.at[c, y, block(lax.rem(pair - s + 4, 4), 64), cols(h)]
        return remote(mine, mine, yas.at[h, s, d - 1], yar.at[h, s, d - 1], at(dy=d))

    @tracked
    def s_gather(h, s):
        mine = z_ref.at[c, :, block(lax.rem(pair - s + 4, 4), 64), cols(h)]
        return remote(mine, mine, sas.at[h, s], sar.at[h, s], at(dc=1))

    def to_y(h):
        s_scatter(h).wait_recv()
        zo_ref[h] += rs_ref[h]
        for s in FAR:
            for d in (2, 1, 3):
                y_scatter(h, s, d).start()

    def to_z(h, s):
        for d in (1, 2, 3):
            y_scatter(h, s, d).wait_recv()
        part = lax.rem(pair + s, 4)
        lines = block(part, 64)
        own = zo_ref[h, block(y * 4 + part, 64), :]
        zy_ref[h, lines, :] = (own + ry_ref[h, 0, lines, :]) + (ry_ref[h, 1, lines, :] + ry_ref[h, 2, lines, :])
        for t in others(s):
            z_scatter(h, s, t).start()

    def back_z(h):
        total = zy_ref[h, block(z, 32), :]
        for s in (0, 1, 3, 2):
            for t in others(s):
                z_scatter(h, s, t).wait_recv()
                total = total + rz_ref[h, 2 * s + t - 1]
        z_ref[c, y, block(z, 32), h * HALF : h * HALF + HALF] = total
        for s in FAR:
            for t in others(s):
                z_gather(h, s, t).start()

    def back_y(h, s):
        for t in others(s):
            z_gather(h, s, t).wait_recv()
        for d in (2, 1, 3):
            y_gather(h, s, d).start()

    def back_s(h, s):
        for d in (1, 2, 3):
            y_gather(h, s, d).wait_recv()
        s_gather(h, s).start()

    @tracked
    def gs_scatter():
        src = gf_ref.at[pl.ds(pl.multiple_of(x * 64 + (1 - c) * 32, 32), 32)]
        return remote(src, gs_ref, gss, gsr, at(dc=1))

    @tracked
    def gy_scatter(d):
        src = g1_ref.at[pl.ds(pl.multiple_of(lax.rem(y + d, NY) * 8, 8), 8)]
        return remote(src, gy_ref.at[d - 1], gys.at[d - 1], gyr.at[d - 1], at(dy=d))

    @tracked
    def gz_all(d):
        mine = gz_ref.at[z]
        return remote(mine, mine, gzs.at[d - 1], gzr.at[d - 1], at(dz=d))

    lines_y = pl.ds(pl.multiple_of(y * 8, 8), 8)

    @tracked
    def g_gather(i):
        mine = gm_ref.at[x, c, lines_y]
        return remote(mine, mine, gas.at[i], gar.at[i], at(dx=flat[i][0], dy=flat[i][1]))

    @tracked
    def gb_gather():
        mine = gm_ref.at[:, c]
        return remote(mine, mine, gbs, gbr, at(dc=1))

    for d in (1, 2, 3):
        x_gather(0, d).wait_recv()
    cross(0, zs_ref, 1 - c)
    s_scatter(0).start()
    cross(0, zo_ref, c)
    for d in (1, 2, 3):
        x_gather(1, d).wait_recv()
    whole = jnp.concatenate([s_ref[0], s_ref[1]], 1)
    gf_ref[...] = lax.dot_general(
        whole, whole, (((0,), (0,)), ((), ())), precision=HIGH, preferred_element_type=F32
    )
    gs_scatter().start()
    to_y(0)
    cross(1, zs_ref, 1 - c)
    s_scatter(1).start()
    gs_scatter().wait_recv()
    g1_ref[...] = gf_ref[pl.ds(pl.multiple_of(x * 64 + c * 32, 32), 32), :] + gs_ref[...]
    for d in (2, 1, 3):
        gy_scatter(d).start()
    cross(1, zo_ref, c)
    to_y(1)
    for d in (1, 2, 3):
        gy_scatter(d).wait_recv()
    gz_ref[z] = (g1_ref[lines_y, :] + gy_ref[0]) + (gy_ref[1] + gy_ref[2])
    for d in (4, 3, 5, 2, 6, 1, 7):
        gz_all(d).start()
    for s in FAR:
        to_z(0, s)
    for d in range(1, NZ):
        gz_all(d).wait_recv()
    total = gz_ref[0]
    for i in range(1, NZ):
        total = total + gz_ref[i]
    gm_ref[x, c, lines_y, :] = total
    for i in range(len(flat)):
        g_gather(i).start()
    x_ref[...] = jnp.where(
        lax.broadcasted_iota(jnp.int32, (WIDTH, WIDTH), 0) == lax.broadcasted_iota(jnp.int32, (WIDTH, WIDTH), 1),
        1.0, 0.0,
    )
    for s in FAR:
        to_z(1, s)
    back_z(0)
    for s in (0, 1, 3, 2):
        back_y(0, s)
    for i in range(len(flat)):
        g_gather(i).wait_recv()
    gb_gather().start()
    gb_gather().wait_recv()
    r_ref[...] = gm_ref[...].reshape(WIDTH, WIDTH)

    hooks = {
        0: ((back_z, 1),),
        3: ((back_y, 1, 0), (back_y, 1, 1), (back_y, 1, 3), (back_y, 1, 2)),
        5: ((back_s, 0, 0), (back_s, 0, 1), (back_s, 0, 3), (back_s, 0, 2)),
    }

    @pl.loop(0, WIDTH // PANEL)
    def _(p):
        for when, steps in hooks.items():

            @pl.when(p == when)
            def _():
                for step, *where in steps:
                    step(*where)

        factor_panel(p, r_ref, x_ref)
        update_below(p, r_ref, x_ref)

    line = lax.broadcasted_iota(jnp.int32, (WIDTH, WIDTH), 0)
    lane = lax.broadcasted_iota(jnp.int32, (WIDTH, WIDTH), 1)
    r_ref[...] = jnp.where(lane >= line, r_ref[...], 0.0)
    for s in (0, 1, 3, 2):
        back_s(1, s)

    copies.drain()


def body(snapshot, test_matrix):
    dma = pltpu.SemaphoreType.DMA
    hbm = pl.BlockSpec(memory_space=pltpu.HBM)
    vmem = pl.BlockSpec(memory_space=pltpu.VMEM)
    cross, factor, inverse = pl.pallas_call(
        kernel,
        out_shape=(
            jax.ShapeDtypeStruct((2, NY, 256, WIDTH), F32),
            jax.ShapeDtypeStruct((WIDTH, WIDTH), F32),
            jax.ShapeDtypeStruct((WIDTH, WIDTH), F32),
        ),
        in_specs=[hbm, hbm],
        out_specs=(vmem, vmem, vmem),
        scratch_shapes=[
            pltpu.VMEM((POINTS, SNAPS), F32),
            pltpu.VMEM((SNAPS, WIDTH), F32),
            pltpu.VMEM((SNAPS, POINTS), F32),
            pltpu.VMEM((2, POINTS, HALF), F32),
            pltpu.VMEM((2, POINTS, HALF), F32),
            pltpu.VMEM((2, 3, SHARE, HALF), F32),
            pltpu.VMEM((2, 1024, HALF), F32),
            pltpu.VMEM((2, 1024, HALF), F32),
            pltpu.VMEM((2, 1024, HALF), F32),
            pltpu.VMEM((2, 3, 256, HALF), F32),
            pltpu.VMEM((2, 256, HALF), F32),
            pltpu.VMEM((2, 7, 32, HALF), F32),
            pltpu.VMEM((WIDTH, WIDTH), F32),
            pltpu.VMEM((32, WIDTH), F32),
            pltpu.VMEM((32, WIDTH), F32),
            pltpu.VMEM((3, 8, WIDTH), F32),
            pltpu.VMEM((8, 8, WIDTH), F32),
            pltpu.VMEM((4, 2, 32, WIDTH), F32),
            dma((2, 8)),
            dma((2, 3)), dma((2, 3)), dma((2, 3)), dma((2, 3)),
            dma((2,)), dma((2,)),
            dma((2, 4, 3)), dma((2, 4, 3)),
            dma((2, 7)), dma((2, 7)), dma((2, 7)), dma((2, 7)),
            dma((2, 4, 3)), dma((2, 4, 3)),
            dma((2, 4)), dma((2, 4)),
            dma, dma,
            dma((3,)), dma((3,)),
            dma((7,)), dma((7,)),
            dma((15,)), dma((15,)),
            dma, dma,
        ],
        compiler_params=pltpu.CompilerParams(
            collective_id=0, has_side_effects=True, vmem_limit_bytes=48 * 1024 * 1024
        ),
        name="range_finder",
    )(*(pltpu.with_memory_space_constraint(value, pltpu.HBM) for value in (snapshot, test_matrix)))
    projected = lax.dot_general(
        cross.reshape(SNAPS, WIDTH), inverse, (((1,), (1,)), ((), ())), precision=HIGH, preferred_element_type=F32
    )
    return projected, factor / jnp.sqrt(jnp.float32(TOTAL))


def solution(mesh):
    return jax.shard_map(
        body,
        mesh=mesh,
        in_specs=(P("rows", "cols"), P("cols", None)),
        out_specs=(P("cols", None), P()),
        check_vma=False,
    )
```

```python
import functools

import jax
import jax.numpy as jnp
from jax import lax
from jax.experimental import pallas as pl
from jax.experimental.pallas import tpu as pltpu
from jax.sharding import PartitionSpec as P

HIGH = lax.Precision.HIGHEST
F32 = jnp.float32
BF16 = jnp.bfloat16
MESH = pl.DeviceIdType.MESH
NZ, NY, NX = 8, 4, 4
POINTS, SNAPS, WIDTH = 384, 2048, 256
HALF = WIDTH // 2
SHARE = POINTS // NX
PANEL = 32
TOTAL = 24576


def three_parts(value):
    first = value.astype(BF16)
    rest = value - first.astype(F32)
    second = rest.astype(BF16)
    third = (rest - second.astype(F32)).astype(BF16)
    return first, second, third


def factor_panel(p, g_ref, x_ref):
    top = pl.multiple_of(p * PANEL, PANEL)
    rows = pl.ds(top, PANEL)
    left, right = g_ref[rows, 0:128], g_ref[rows, 128:256]
    own = jnp.where(p < 4, left, right)
    own = pltpu.roll(own, lax.rem(128 - lax.rem(top, 128), 128), 1)
    x_left, x_right = x_ref[rows, 0:128], x_ref[rows, 128:256]
    wide = (left, right, x_left, x_right, own)
    tiles = [[part[8 * g : 8 * g + 8] for part in wide] for g in range(4)]
    sub = lax.broadcasted_iota(jnp.int32, (8, 128), 0)
    for b in range(4):
        column = {}
        for k in range(8):
            for g in range(b, 4):
                lane = tiles[g][4][:, 8 * b + k : 8 * b + k + 1]
                column[g, k] = jnp.broadcast_to(lane, (8, 128))
        for k in range(8):
            scale = lax.rsqrt(jnp.broadcast_to(column[b, k][k : k + 1, :], (8, 128)))
            low = {g: column[g, k] * scale for g in range(b, 4)}
            for m in range(k + 1, 8):
                entry = jnp.broadcast_to(low[b][m : m + 1, :], (8, 128))
                for g in range(b, 4):
                    column[g, m] = column[g, m] - low[g] * entry
            below = jnp.where(sub <= k, 0.0, low[b])
            for w in range(5):
                row = jnp.broadcast_to(tiles[b][w][k : k + 1, :], (8, 128)) * scale
                tiles[b][w] = jnp.where(sub == k, row, tiles[b][w] - below * row)
                for g in range(b + 1, 4):
                    tiles[g][w] = tiles[g][w] - low[g] * row
    for g in range(4):
        lines = pl.ds(top + 8 * g, 8)
        g_ref[lines, 0:128], g_ref[lines, 128:256] = tiles[g][0], tiles[g][1]
        x_ref[lines, 0:128], x_ref[lines, 128:256] = tiles[g][2], tiles[g][3]


def update_below(p, g_ref, x_ref):
    top = pl.multiple_of(p * PANEL, PANEL)
    g, x = g_ref[pl.ds(top, PANEL), :], x_ref[pl.ds(top, PANEL), :]
    lane = lax.broadcasted_iota(jnp.int32, (PANEL, WIDTH), 1)
    a, b, c = three_parts(jnp.where(lane >= top + PANEL, g, 0.0))
    lhs = jnp.concatenate([a, a, b, a, c, b], 0)
    dims = (((0,), (0,)), ((), ()))
    for ref, value in ((g_ref, g), (x_ref, x)):
        a, b, c = three_parts(value)
        rhs = jnp.concatenate([a, b, a, c, a, b], 0)
        ref[...] -= lax.dot_general(lhs, rhs, dims, preferred_element_type=F32)


class Copies:
    def __init__(self):
        self.open = {}

    def tracked(self, make):
        return lambda *where: Copy(self.open, make, where)

    def drain(self):
        for (make, where), sides in self.open.items():
            copy = make(*where)
            for side in sides:
                getattr(copy, side)()
        self.open = {}


class Copy:
    def __init__(self, open_copies, make, where):
        self.open, self.key, self.copy = open_copies, (make, where), make(*where)

    def start(self):
        self.copy.start()
        self.open[self.key] = ["wait_recv", "wait_send"]

    def wait_recv(self):
        self.copy.wait_recv()
        self.open[self.key].remove("wait_recv")

    def wait_send(self):
        self.copy.wait_send()
        self.open[self.key].remove("wait_send")


def kernel(
    a_hbm, t_hbm, z_ref, r_ref, x_ref,
    a_ref, t_ref, at_ref, p_ref, s_ref, rx_ref, zs_ref, zo_ref, rs_ref, ry_ref, zy_ref, rz_ref,
    gf_ref, gs_ref, g1_ref, gy_ref, gz_ref, gm_ref,
    load, xs, xr, xas, xar, ss, sr, ys, yr, zs, zr, zas, zar, yas, yar, sas, sar,
    gss, gsr, gys, gyr, gzs, gzr, gas, gar, gcs, gcr, gbs, gbr,
):
    row, x = lax.axis_index("rows"), lax.axis_index("cols")
    c, y, z = lax.rem(row, 2), lax.rem(row // 2, NY), row // (2 * NY)

    def at(dz=0, dy=0, dx=0, dc=0):
        zz, yy = lax.rem(z + dz, NZ), lax.rem(y + dy, NY)
        xx, cc = lax.rem(x + dx, NX), lax.rem(c + dc, 2)
        return ((zz * NY + yy) * 2 + cc, xx)

    def remote(src, dst, send, recv, device):
        return pltpu.make_async_remote_copy(
            src_ref=src, dst_ref=dst, send_sem=send, recv_sem=recv, device_id=device, device_id_type=MESH
        )

    copies = Copies()
    tracked = copies.tracked

    def load_a(k):
        part = pl.ds(k * 256, 256)
        return pltpu.make_async_copy(a_hbm.at[:, part], a_ref.at[:, part], load.at[0, k])

    def load_t(k):
        part = pl.ds(k * 256, 256)
        return pltpu.make_async_copy(t_hbm.at[part, :], t_ref.at[part, :], load.at[1, k])

    for k in range(8):
        load_a(k).start()
        load_t(k).start()
    barrier = pltpu.get_barrier_semaphore()
    friends = [at(dc=1)] + [at(dz=d) for d in range(1, NZ)] + [at(dy=d) for d in (1, 2, 3)] + [at(dx=d) for d in (1, 2, 3)]
    for friend in friends:
        pl.semaphore_signal(barrier, inc=1, device_id=friend, device_id_type=MESH)

    def share(index):
        return pl.ds(pl.multiple_of(index * SHARE, SHARE), SHARE)

    @tracked
    def x_scatter(h, d):
        src = p_ref.at[h, share(lax.rem(x + d, NX))]
        return remote(src, rx_ref.at[h, d - 1], xs.at[h, d - 1], xr.at[h, d - 1], at(dx=d))

    for group in ((2, 1), (3, 0)):
        for k in range(8):
            if group[0] == 2:
                load_a(k).wait()
                load_t(k).wait()
            lines = [share(lax.rem(x + d, NX)) for d in group]
            part = jnp.dot(
                jnp.concatenate([a_ref[line, k * 256 : k * 256 + 256] for line in lines], 0),
                t_ref[k * 256 : k * 256 + 256, :],
                precision=HIGH, preferred_element_type=F32,
            )
            for i, line in enumerate(lines):
                for h in range(2):
                    piece = part[i * SHARE : i * SHARE + SHARE, h * HALF : h * HALF + HALF]
                    p_ref[h, line, :] = piece if k == 0 else p_ref[h, line, :] + piece
        if group[0] == 2:
            pl.semaphore_wait(barrier, len(friends))
        for h in range(2):
            for d in group:
                if d:
                    x_scatter(h, d).start()

    @tracked
    def x_gather(h, d):
        mine = s_ref.at[h, share(x)]
        return remote(mine, mine, xas.at[h, d - 1], xar.at[h, d - 1], at(dx=d))

    for k in range(8):
        at_ref[k * 256 : k * 256 + 256, :] = a_ref[:, k * 256 : k * 256 + 256].T
    for h in range(2):
        for d in (1, 2, 3):
            x_scatter(h, d).wait_recv()
        s_ref[h, share(x), :] = (p_ref[h, share(x), :] + rx_ref[h, 0]) + (rx_ref[h, 1] + rx_ref[h, 2])
        for d in (2, 1, 3):
            x_gather(h, d).start()

    def cross(h, out_ref, core):
        sketch = s_ref[h]

        @pl.loop(0, 4)
        def _(i):
            lines = pl.ds(pl.multiple_of(core * 1024 + i * 256, 256), 256)
            out_ref[h, pl.ds(pl.multiple_of(i * 256, 256), 256), :] = jnp.dot(
                at_ref[lines, :], sketch, precision=HIGH, preferred_element_type=F32
            )

    @tracked
    def s_scatter(h):
        return remote(zs_ref.at[h], rs_ref.at[h], ss.at[h], sr.at[h], at(dc=1))

    pair, bit = z // 2, lax.rem(z, 2)
    FAR = (2, 1, 3, 0)

    def further(s, t):
        return 2 * lax.rem(pair + s, 4) + lax.rem(bit + t, 2)

    def block(index, size):
        return pl.ds(pl.multiple_of(index * size, size), size)

    def others(s):
        return (1,) if s == 0 else (0, 1)

    @tracked
    def y_scatter(h, s, d):
        part = lax.rem(pair + s, 4)
        src = zo_ref.at[h, block(lax.rem(y + d, NY) * 4 + part, 64)]
        return remote(src, ry_ref.at[h, d - 1, block(part, 64)], ys.at[h, s, d - 1], yr.at[h, s, d - 1], at(dy=d))

    @tracked
    def z_scatter(h, s, t):
        src = zy_ref.at[h, block(further(s, t), 32)]
        i = 2 * s + t - 1
        return remote(src, rz_ref.at[h, i], zs.at[h, i], zr.at[h, i], at(dz=further(s, t) - z + NZ))

    @tracked
    def z_gather(h, s, t):
        mine = z_ref.at[h, c, y, block(z, 32)]
        i = 2 * s + t - 1
        return remote(mine, mine, zas.at[h, i], zar.at[h, i], at(dz=further(s, t) - z + NZ))

    @tracked
    def y_gather(h, s, d):
        mine = z_ref.at[h, c, y, block(lax.rem(pair - s + 4, 4), 64)]
        return remote(mine, mine, yas.at[h, s, d - 1], yar.at[h, s, d - 1], at(dy=d))

    @tracked
    def s_gather(h, s):
        mine = z_ref.at[h, c, :, block(lax.rem(pair - s + 4, 4), 64)]
        return remote(mine, mine, sas.at[h, s], sar.at[h, s], at(dc=1))

    def to_y(h):
        s_scatter(h).wait_recv()
        zo_ref[h] += rs_ref[h]
        for s in FAR:
            for d in (2, 1, 3):
                y_scatter(h, s, d).start()

    def to_z(h, s):
        for d in (1, 2, 3):
            y_scatter(h, s, d).wait_recv()
        part = lax.rem(pair + s, 4)
        lines = block(part, 64)
        own = zo_ref[h, block(y * 4 + part, 64), :]
        zy_ref[h, lines, :] = (own + ry_ref[h, 0, lines, :]) + (ry_ref[h, 1, lines, :] + ry_ref[h, 2, lines, :])
        for t in others(s):
            z_scatter(h, s, t).start()

    def back_z(h):
        total = zy_ref[h, block(z, 32), :]
        for s in (0, 1, 3, 2):
            for t in others(s):
                z_scatter(h, s, t).wait_recv()
                total = total + rz_ref[h, 2 * s + t - 1]
        z_ref[h, c, y, block(z, 32), :] = total
        for s in FAR:
            for t in others(s):
                z_gather(h, s, t).start()

    def back_y(h, s):
        for t in others(s):
            z_gather(h, s, t).wait_recv()
        for d in (2, 1, 3):
            y_gather(h, s, d).start()

    def back_s(h, s):
        for d in (1, 2, 3):
            y_gather(h, s, d).wait_recv()
        s_gather(h, s).start()

    @tracked
    def gs_scatter():
        src = gf_ref.at[pl.ds(pl.multiple_of(x * 64 + (1 - c) * 32, 32), 32)]
        return remote(src, gs_ref, gss, gsr, at(dc=1))

    @tracked
    def gz_scatter(d):
        src = g1_ref.at[lax.rem(z + d, NZ)]
        return remote(src, gz_ref.at[d - 1], gzs.at[d - 1], gzr.at[d - 1], at(dz=d))

    @tracked
    def gy_all(d):
        mine = gy_ref.at[y]
        return remote(mine, mine, gys.at[d - 1], gyr.at[d - 1], at(dy=d))

    @tracked
    def gx_gather(d):
        mine = gm_ref.at[x, c, z]
        return remote(mine, mine, gas.at[d - 1], gar.at[d - 1], at(dx=d))

    @tracked
    def gz_gather(d):
        mine = gm_ref.at[:, c, z]
        return remote(mine, mine, gcs.at[d - 1], gcr.at[d - 1], at(dz=d))

    @tracked
    def gb_gather():
        mine = gm_ref.at[:, c]
        return remote(mine, mine, gbs, gbr, at(dc=1))

    for d in (1, 2, 3):
        x_gather(0, d).wait_recv()
    cross(0, zs_ref, 1 - c)
    s_scatter(0).start()
    cross(0, zo_ref, c)
    for d in (1, 2, 3):
        x_gather(1, d).wait_recv()
    whole = jnp.concatenate([s_ref[0], s_ref[1]], 1)
    gf_ref[...] = lax.dot_general(
        whole, whole, (((0,), (0,)), ((), ())), precision=HIGH, preferred_element_type=F32
    )
    gs_scatter().start()
    to_y(0)
    cross(1, zs_ref, 1 - c)
    s_scatter(1).start()
    x_ref[...] = jnp.where(
        lax.broadcasted_iota(jnp.int32, (WIDTH, WIDTH), 0) == lax.broadcasted_iota(jnp.int32, (WIDTH, WIDTH), 1),
        1.0, 0.0,
    )
    gs_scatter().wait_recv()
    total = gf_ref[pl.ds(pl.multiple_of(x * 64 + c * 32, 32), 32), :] + gs_ref[...]
    for i in range(2):
        g1_ref[4 * i : 4 * i + 4] = total[:, i * HALF : i * HALF + HALF].reshape(4, 8, HALF)
    for d in (4, 3, 5, 2, 6, 1, 7):
        gz_scatter(d).start()
    cross(1, zo_ref, c)
    to_z(0, 2)
    total = g1_ref[z]
    for d in range(1, NZ):
        gz_scatter(d).wait_recv()
        total = total + gz_ref[d - 1]
    gy_ref[y] = total
    for d in (2, 1, 3):
        gy_all(d).start()
    to_y(1)
    for s in (1, 3, 0):
        to_z(0, s)
    for d in (1, 2, 3):
        gy_all(d).wait_recv()
    gm_ref[x, c, z] = (gy_ref[0] + gy_ref[1]) + (gy_ref[2] + gy_ref[3])
    for d in (2, 1, 3):
        gx_gather(d).start()
    to_z(1, 2)
    to_z(1, 1)
    for d in (1, 2, 3):
        gx_gather(d).wait_recv()
    for d in (4, 3, 5, 2, 6, 1, 7):
        gz_gather(d).start()
    back_z(0)
    to_z(1, 3)
    to_z(1, 0)
    for d in range(1, NZ):
        gz_gather(d).wait_recv()
    gb_gather().start()
    back_y(0, 0)
    gb_gather().wait_recv()
    for i in range(2):
        r_ref[:, i * HALF : i * HALF + HALF] = gm_ref[:, :, 4 * i : 4 * i + 4].reshape(WIDTH, HALF)

    hooks = {
        0: ((back_y, 0, 1), (back_y, 0, 3)),
        1: ((back_y, 0, 2), (back_z, 1)),
        4: ((back_y, 1, 0), (back_y, 1, 1), (back_y, 1, 3)),
        5: ((back_y, 1, 2), (back_s, 0, 0)),
        7: ((back_s, 0, 1), (back_s, 0, 3), (back_s, 0, 2)),
    }

    @pl.loop(0, WIDTH // PANEL)
    def _(p):
        for when, steps in hooks.items():

            @pl.when(p == when)
            def _():
                for step, *where in steps:
                    step(*where)

        factor_panel(p, r_ref, x_ref)
        update_below(p, r_ref, x_ref)

    line = lax.broadcasted_iota(jnp.int32, (WIDTH, WIDTH), 0)
    lane = lax.broadcasted_iota(jnp.int32, (WIDTH, WIDTH), 1)
    r_ref[...] = jnp.where(lane >= line, r_ref[...], 0.0)
    x_ref[...] = x_ref[...].T
    for s in (0, 1, 3, 2):
        back_s(1, s)

    copies.drain()


def finish(z_ref, w_ref, r_ref, out_hbm, triangle_hbm, out_ref, triangle_ref, sem):
    triangle_ref[...] = r_ref[...] * (TOTAL**-0.5)
    copies = [pltpu.make_async_copy(triangle_ref, triangle_hbm, sem.at[4])]
    copies[0].start()
    for i in range(4):
        lines = pl.ds(i * 512, 512)
        out_ref[lines, :] = jnp.dot(
            jnp.concatenate([z_ref[0, lines, :], z_ref[1, lines, :]], 1), w_ref[...],
            precision=HIGH, preferred_element_type=F32,
        )
        copies.append(pltpu.make_async_copy(out_ref.at[lines], out_hbm.at[lines], sem.at[i]))
        copies[-1].start()
    for copy in copies:
        copy.wait()


def body(snapshot, test_matrix):
    dma = pltpu.SemaphoreType.DMA
    hbm = pl.BlockSpec(memory_space=pltpu.HBM)
    vmem = pl.BlockSpec(memory_space=pltpu.VMEM)
    cross, factor, inverse = pl.pallas_call(
        kernel,
        out_shape=(
            jax.ShapeDtypeStruct((2, 2, NY, 256, HALF), F32),
            jax.ShapeDtypeStruct((WIDTH, WIDTH), F32),
            jax.ShapeDtypeStruct((WIDTH, WIDTH), F32),
        ),
        in_specs=[hbm, hbm],
        out_specs=(vmem, vmem, vmem),
        scratch_shapes=[
            pltpu.VMEM((POINTS, SNAPS), F32),
            pltpu.VMEM((SNAPS, WIDTH), F32),
            pltpu.VMEM((SNAPS, POINTS), F32),
            pltpu.VMEM((2, POINTS, HALF), F32),
            pltpu.VMEM((2, POINTS, HALF), F32),
            pltpu.VMEM((2, 3, SHARE, HALF), F32),
            pltpu.VMEM((2, 1024, HALF), F32),
            pltpu.VMEM((2, 1024, HALF), F32),
            pltpu.VMEM((2, 1024, HALF), F32),
            pltpu.VMEM((2, 3, 256, HALF), F32),
            pltpu.VMEM((2, 256, HALF), F32),
            pltpu.VMEM((2, 7, 32, HALF), F32),
            pltpu.VMEM((WIDTH, WIDTH), F32),
            pltpu.VMEM((32, WIDTH), F32),
            pltpu.VMEM((8, 8, HALF), F32),
            pltpu.VMEM((4, 8, HALF), F32),
            pltpu.VMEM((7, 8, HALF), F32),
            pltpu.VMEM((4, 2, 8, 8, HALF), F32),
            dma((2, 8)),
            dma((2, 3)), dma((2, 3)), dma((2, 3)), dma((2, 3)),
            dma((2,)), dma((2,)),
            dma((2, 4, 3)), dma((2, 4, 3)),
            dma((2, 7)), dma((2, 7)), dma((2, 7)), dma((2, 7)),
            dma((2, 4, 3)), dma((2, 4, 3)),
            dma((2, 4)), dma((2, 4)),
            dma, dma,
            dma((3,)), dma((3,)),
            dma((7,)), dma((7,)),
            dma((3,)), dma((3,)),
            dma((7,)), dma((7,)),
            dma, dma,
        ],
        compiler_params=pltpu.CompilerParams(
            collective_id=0, has_side_effects=True, vmem_limit_bytes=48 * 1024 * 1024
        ),
        name="range_finder",
    )(*(pltpu.with_memory_space_constraint(value, pltpu.HBM) for value in (snapshot, test_matrix)))
    return pl.pallas_call(
        finish,
        out_shape=(
            jax.ShapeDtypeStruct((SNAPS, WIDTH), F32),
            jax.ShapeDtypeStruct((WIDTH, WIDTH), F32),
        ),
        in_specs=[vmem, vmem, vmem],
        out_specs=(hbm, hbm),
        scratch_shapes=[
            pltpu.VMEM((SNAPS, WIDTH), F32),
            pltpu.VMEM((WIDTH, WIDTH), F32),
            dma((5,)),
        ],
        compiler_params=pltpu.CompilerParams(vmem_limit_bytes=16 * 1024 * 1024),
        name="final_product",
    )(cross.reshape(2, SNAPS, HALF), inverse, factor)


def solution(mesh):
    return jax.shard_map(
        body,
        mesh=mesh,
        in_specs=(P("rows", "cols"), P("cols", None)),
        out_specs=(P("cols", None), P()),
        check_vma=False,
    )
```

```python
import functools

import jax
import jax.numpy as jnp
from jax import lax
from jax.experimental import pallas as pl
from jax.experimental.pallas import tpu as pltpu
from jax.sharding import PartitionSpec as P

HIGH = lax.Precision.HIGHEST
F32 = jnp.float32
BF16 = jnp.bfloat16
MESH = pl.DeviceIdType.MESH
NZ, NY, NX = 8, 4, 4
POINTS, SNAPS, WIDTH = 384, 2048, 256
HALF = WIDTH // 2
SHARE = POINTS // NX
PANEL = 32
TOTAL = 24576


def three_parts(value):
    first = value.astype(BF16)
    rest = value - first.astype(F32)
    second = rest.astype(BF16)
    third = (rest - second.astype(F32)).astype(BF16)
    return first, second, third


def factor_panel(p, g_ref, x_ref):
    top = pl.multiple_of(p * PANEL, PANEL)
    rows = pl.ds(top, PANEL)
    left, right = g_ref[rows, 0:128], g_ref[rows, 128:256]
    own = jnp.where(p < 4, left, right)
    own = pltpu.roll(own, lax.rem(128 - lax.rem(top, 128), 128), 1)
    x_left, x_right = x_ref[rows, 0:128], x_ref[rows, 128:256]
    wide = (left, right, x_left, x_right, own)
    tiles = [[part[8 * g : 8 * g + 8] for part in wide] for g in range(4)]
    sub = lax.broadcasted_iota(jnp.int32, (8, 128), 0)
    for b in range(4):
        column = {}
        for k in range(8):
            for g in range(b, 4):
                lane = tiles[g][4][:, 8 * b + k : 8 * b + k + 1]
                column[g, k] = jnp.broadcast_to(lane, (8, 128))
        for k in range(8):
            scale = lax.rsqrt(jnp.broadcast_to(column[b, k][k : k + 1, :], (8, 128)))
            low = {g: column[g, k] * scale for g in range(b, 4)}
            for m in range(k + 1, 8):
                entry = jnp.broadcast_to(low[b][m : m + 1, :], (8, 128))
                for g in range(b, 4):
                    column[g, m] = column[g, m] - low[g] * entry
            below = jnp.where(sub <= k, 0.0, low[b])
            for w in range(5):
                row = jnp.broadcast_to(tiles[b][w][k : k + 1, :], (8, 128)) * scale
                tiles[b][w] = jnp.where(sub == k, row, tiles[b][w] - below * row)
                for g in range(b + 1, 4):
                    tiles[g][w] = tiles[g][w] - low[g] * row
    for g in range(4):
        lines = pl.ds(top + 8 * g, 8)
        g_ref[lines, 0:128], g_ref[lines, 128:256] = tiles[g][0], tiles[g][1]
        x_ref[lines, 0:128], x_ref[lines, 128:256] = tiles[g][2], tiles[g][3]


def update_below(p, g_ref, x_ref):
    top = pl.multiple_of(p * PANEL, PANEL)
    g, x = g_ref[pl.ds(top, PANEL), :], x_ref[pl.ds(top, PANEL), :]
    lane = lax.broadcasted_iota(jnp.int32, (PANEL, WIDTH), 1)
    a, b, c = three_parts(jnp.where(lane >= top + PANEL, g, 0.0))
    lhs = jnp.concatenate([a, a, b, a, c, b], 0)
    dims = (((0,), (0,)), ((), ()))
    for ref, value in ((g_ref, g), (x_ref, x)):
        a, b, c = three_parts(value)
        rhs = jnp.concatenate([a, b, a, c, a, b], 0)
        ref[...] -= lax.dot_general(lhs, rhs, dims, preferred_element_type=F32)


class Copies:
    def __init__(self):
        self.open = {}

    def tracked(self, make):
        return lambda *where: Copy(self.open, make, where)

    def drain(self):
        for (make, where), sides in self.open.items():
            copy = make(*where)
            for side in sides:
                getattr(copy, side)()
        self.open = {}


class Copy:
    def __init__(self, open_copies, make, where):
        self.open, self.key, self.copy = open_copies, (make, where), make(*where)

    def start(self):
        self.copy.start()
        self.open[self.key] = ["wait_recv", "wait_send"]

    def wait_recv(self):
        self.copy.wait_recv()
        self.open[self.key].remove("wait_recv")

    def wait_send(self):
        self.copy.wait_send()
        self.open[self.key].remove("wait_send")


def kernel(
    a_hbm, t_hbm, z_ref, r_ref, x_ref,
    a_ref, t_ref, at_ref, p_ref, s_ref, rx_ref, zs_ref, zo_ref, rs_ref, ry_ref, zy_ref, rz_ref,
    gf_ref, gs_ref, g1_ref, gy_ref, gz_ref, gm_ref,
    load, xs, xr, xas, xar, ss, sr, ys, yr, zs, zr, zas, zar, yas, yar, sas, sar,
    gss, gsr, gys, gyr, gzs, gzr, gas, gar, gcs, gcr, gbs, gbr,
):
    row, x = lax.axis_index("rows"), lax.axis_index("cols")
    c, y, z = lax.rem(row, 2), lax.rem(row // 2, NY), row // (2 * NY)

    def at(dz=0, dy=0, dx=0, dc=0):
        zz, yy = lax.rem(z + dz, NZ), lax.rem(y + dy, NY)
        xx, cc = lax.rem(x + dx, NX), lax.rem(c + dc, 2)
        return ((zz * NY + yy) * 2 + cc, xx)

    def remote(src, dst, send, recv, device):
        return pltpu.make_async_remote_copy(
            src_ref=src, dst_ref=dst, send_sem=send, recv_sem=recv, device_id=device, device_id_type=MESH
        )

    copies = Copies()
    tracked = copies.tracked

    def load_a(k):
        part = pl.ds(k * 256, 256)
        return pltpu.make_async_copy(a_hbm.at[:, part], a_ref.at[:, part], load.at[0, k])

    def load_t(k):
        part = pl.ds(k * 256, 256)
        return pltpu.make_async_copy(t_hbm.at[part, :], t_ref.at[part, :], load.at[1, k])

    for k in range(8):
        load_a(k).start()
        load_t(k).start()
    barrier = pltpu.get_barrier_semaphore()
    friends = [at(dc=1)] + [at(dz=d) for d in range(1, NZ)] + [at(dy=d) for d in (1, 2, 3)] + [at(dx=d) for d in (1, 2, 3)]
    for friend in friends:
        pl.semaphore_signal(barrier, inc=1, device_id=friend, device_id_type=MESH)

    def share(index):
        return pl.ds(pl.multiple_of(index * SHARE, SHARE), SHARE)

    @tracked
    def x_scatter(h, d):
        src = p_ref.at[h, share(lax.rem(x + d, NX))]
        return remote(src, rx_ref.at[h, d - 1], xs.at[h, d - 1], xr.at[h, d - 1], at(dx=d))

    for group in ((2, 1), (3, 0)):
        for k in range(8):
            if group[0] == 2:
                load_a(k).wait()
                load_t(k).wait()
            lines = [share(lax.rem(x + d, NX)) for d in group]
            part = jnp.dot(
                jnp.concatenate([a_ref[line, k * 256 : k * 256 + 256] for line in lines], 0),
                t_ref[k * 256 : k * 256 + 256, :],
                precision=HIGH, preferred_element_type=F32,
            )
            for i, line in enumerate(lines):
                for h in range(2):
                    piece = part[i * SHARE : i * SHARE + SHARE, h * HALF : h * HALF + HALF]
                    p_ref[h, line, :] = piece if k == 0 else p_ref[h, line, :] + piece
        if group[0] == 2:
            pl.semaphore_wait(barrier, len(friends))
        for h in range(2):
            for d in group:
                if d:
                    x_scatter(h, d).start()

    @tracked
    def x_gather(h, d):
        mine = s_ref.at[h, share(x)]
        return remote(mine, mine, xas.at[h, d - 1], xar.at[h, d - 1], at(dx=d))

    for k in range(8):
        at_ref[k * 256 : k * 256 + 256, :] = a_ref[:, k * 256 : k * 256 + 256].T
    for h in range(2):
        for d in (1, 2, 3):
            x_scatter(h, d).wait_recv()
        s_ref[h, share(x), :] = (p_ref[h, share(x), :] + rx_ref[h, 0]) + (rx_ref[h, 1] + rx_ref[h, 2])
        for d in (2, 1, 3):
            x_gather(h, d).start()

    def cross(h, out_ref, core):
        s1, s2, s3 = three_parts(s_ref[h])
        near = jnp.concatenate([s1, s2], 1)
        rest = jnp.concatenate([s3, s1], 0)

        @pl.loop(0, 4)
        def _(i):
            lines = pl.ds(pl.multiple_of(core * 1024 + i * 256, 256), 256)
            a1, a2, a3 = three_parts(at_ref[lines, :])
            one = jnp.dot(a1, near, preferred_element_type=F32)
            two = jnp.dot(a2, near, preferred_element_type=F32)
            out = jnp.dot(jnp.concatenate([a1, a3], 1), rest, preferred_element_type=F32)
            out = (out + two[:, HALF:]) + ((two[:, :HALF] + one[:, HALF:]) + one[:, :HALF])
            out_ref[h, pl.ds(pl.multiple_of(i * 256, 256), 256), :] = out

    @tracked
    def s_scatter(h):
        return remote(zs_ref.at[h], rs_ref.at[h], ss.at[h], sr.at[h], at(dc=1))

    pair, bit = z // 2, lax.rem(z, 2)
    FAR = (2, 1, 3, 0)

    def further(s, t):
        return 2 * lax.rem(pair + s, 4) + lax.rem(bit + t, 2)

    def block(index, size):
        return pl.ds(pl.multiple_of(index * size, size), size)

    def others(s):
        return (1,) if s == 0 else (0, 1)

    @tracked
    def y_scatter(h, s, d):
        part = lax.rem(pair + s, 4)
        src = zo_ref.at[h, block(lax.rem(y + d, NY) * 4 + part, 64)]
        return remote(src, ry_ref.at[h, d - 1, block(part, 64)], ys.at[h, s, d - 1], yr.at[h, s, d - 1], at(dy=d))

    @tracked
    def z_scatter(h, s, t):
        src = zy_ref.at[h, block(further(s, t), 32)]
        i = 2 * s + t - 1
        return remote(src, rz_ref.at[h, i], zs.at[h, i], zr.at[h, i], at(dz=further(s, t) - z + NZ))

    @tracked
    def z_gather(h, s, t):
        mine = z_ref.at[h, c, y, block(z, 32)]
        i = 2 * s + t - 1
        return remote(mine, mine, zas.at[h, i], zar.at[h, i], at(dz=further(s, t) - z + NZ))

    @tracked
    def y_gather(h, s, d):
        mine = z_ref.at[h, c, y, block(lax.rem(pair - s + 4, 4), 64)]
        return remote(mine, mine, yas.at[h, s, d - 1], yar.at[h, s, d - 1], at(dy=d))

    @tracked
    def s_gather(h, s):
        mine = z_ref.at[h, c, :, block(lax.rem(pair - s + 4, 4), 64)]
        return remote(mine, mine, sas.at[h, s], sar.at[h, s], at(dc=1))

    def to_y(h):
        s_scatter(h).wait_recv()
        zo_ref[h] += rs_ref[h]
        for s in FAR:
            for d in (2, 1, 3):
                y_scatter(h, s, d).start()

    def to_z(h, s):
        for d in (1, 2, 3):
            y_scatter(h, s, d).wait_recv()
        part = lax.rem(pair + s, 4)
        lines = block(part, 64)
        own = zo_ref[h, block(y * 4 + part, 64), :]
        zy_ref[h, lines, :] = (own + ry_ref[h, 0, lines, :]) + (ry_ref[h, 1, lines, :] + ry_ref[h, 2, lines, :])
        for t in others(s):
            z_scatter(h, s, t).start()

    def back_z(h):
        total = zy_ref[h, block(z, 32), :]
        for s in (0, 1, 3, 2):
            for t in others(s):
                z_scatter(h, s, t).wait_recv()
                total = total + rz_ref[h, 2 * s + t - 1]
        z_ref[h, c, y, block(z, 32), :] = total
        for s in FAR:
            for t in others(s):
                z_gather(h, s, t).start()

    def back_y(h, s):
        for t in others(s):
            z_gather(h, s, t).wait_recv()
        for d in (2, 1, 3):
            y_gather(h, s, d).start()

    def back_s(h, s):
        for d in (1, 2, 3):
            y_gather(h, s, d).wait_recv()
        s_gather(h, s).start()

    @tracked
    def gs_scatter():
        src = gf_ref.at[pl.ds(pl.multiple_of(x * 64 + (1 - c) * 32, 32), 32)]
        return remote(src, gs_ref, gss, gsr, at(dc=1))

    @tracked
    def gz_scatter(d):
        src = g1_ref.at[lax.rem(z + d, NZ)]
        return remote(src, gz_ref.at[d - 1], gzs.at[d - 1], gzr.at[d - 1], at(dz=d))

    @tracked
    def gy_all(d):
        mine = gy_ref.at[y]
        return remote(mine, mine, gys.at[d - 1], gyr.at[d - 1], at(dy=d))

    @tracked
    def gx_gather(d):
        mine = gm_ref.at[x, c, z]
        return remote(mine, mine, gas.at[d - 1], gar.at[d - 1], at(dx=d))

    @tracked
    def gz_gather(d):
        mine = gm_ref.at[:, c, z]
        return remote(mine, mine, gcs.at[d - 1], gcr.at[d - 1], at(dz=d))

    @tracked
    def gb_gather():
        mine = gm_ref.at[:, c]
        return remote(mine, mine, gbs, gbr, at(dc=1))

    for d in (1, 2, 3):
        x_gather(0, d).wait_recv()
    cross(0, zs_ref, 1 - c)
    s_scatter(0).start()
    cross(0, zo_ref, c)
    for d in (1, 2, 3):
        x_gather(1, d).wait_recv()
    whole = jnp.concatenate([s_ref[0], s_ref[1]], 1)
    gf_ref[...] = lax.dot_general(
        whole, whole, (((0,), (0,)), ((), ())), precision=HIGH, preferred_element_type=F32
    )
    gs_scatter().start()
    to_y(0)
    cross(1, zs_ref, 1 - c)
    s_scatter(1).start()
    x_ref[...] = jnp.where(
        lax.broadcasted_iota(jnp.int32, (WIDTH, WIDTH), 0) == lax.broadcasted_iota(jnp.int32, (WIDTH, WIDTH), 1),
        1.0, 0.0,
    )
    gs_scatter().wait_recv()
    total = gf_ref[pl.ds(pl.multiple_of(x * 64 + c * 32, 32), 32), :] + gs_ref[...]
    for i in range(2):
        g1_ref[4 * i : 4 * i + 4] = total[:, i * HALF : i * HALF + HALF].reshape(4, 8, HALF)
    for d in (4, 3, 5, 2, 6, 1, 7):
        gz_scatter(d).start()
    cross(1, zo_ref, c)
    to_z(0, 2)
    total = g1_ref[z]
    for d in range(1, NZ):
        gz_scatter(d).wait_recv()
        total = total + gz_ref[d - 1]
    gy_ref[y] = total
    for d in (2, 1, 3):
        gy_all(d).start()
    to_y(1)
    for s in (1, 3, 0):
        to_z(0, s)
    for d in (1, 2, 3):
        gy_all(d).wait_recv()
    gm_ref[x, c, z] = (gy_ref[0] + gy_ref[1]) + (gy_ref[2] + gy_ref[3])
    for d in (2, 1, 3):
        gx_gather(d).start()
    to_z(1, 2)
    to_z(1, 1)
    for d in (1, 2, 3):
        gx_gather(d).wait_recv()
    for d in (4, 3, 5, 2, 6, 1, 7):
        gz_gather(d).start()
    back_z(0)
    to_z(1, 3)
    to_z(1, 0)
    for d in range(1, NZ):
        gz_gather(d).wait_recv()
    gb_gather().start()
    back_y(0, 0)
    gb_gather().wait_recv()
    for i in range(2):
        r_ref[:, i * HALF : i * HALF + HALF] = gm_ref[:, :, 4 * i : 4 * i + 4].reshape(WIDTH, HALF)

    hooks = {
        0: ((back_y, 0, 1), (back_y, 0, 3)),
        1: ((back_y, 0, 2), (back_z, 1)),
        4: ((back_y, 1, 0), (back_y, 1, 1), (back_y, 1, 3)),
        5: ((back_y, 1, 2), (back_s, 0, 0)),
        7: ((back_s, 0, 1), (back_s, 0, 3), (back_s, 0, 2)),
    }

    @pl.loop(0, WIDTH // PANEL)
    def _(p):
        for when, steps in hooks.items():

            @pl.when(p == when)
            def _():
                for step, *where in steps:
                    step(*where)

        factor_panel(p, r_ref, x_ref)
        update_below(p, r_ref, x_ref)

    line = lax.broadcasted_iota(jnp.int32, (WIDTH, WIDTH), 0)
    lane = lax.broadcasted_iota(jnp.int32, (WIDTH, WIDTH), 1)
    r_ref[...] = jnp.where(lane >= line, r_ref[...], 0.0)
    x_ref[...] = x_ref[...].T
    for s in (0, 1, 3, 2):
        back_s(1, s)

    copies.drain()


def finish(z_ref, w_ref, r_ref, out_hbm, triangle_hbm, out_ref, triangle_ref, sem):
    triangle_ref[...] = r_ref[...] * (TOTAL**-0.5)
    copies = [pltpu.make_async_copy(triangle_ref, triangle_hbm, sem.at[4])]
    copies[0].start()
    w1, w2, w3 = three_parts(w_ref[...])
    low = jnp.concatenate([w3, w1, w2], 0)
    for i in range(4):
        lines = pl.ds(i * 512, 512)
        z1, z2, z3 = three_parts(jnp.concatenate([z_ref[0, lines, :], z_ref[1, lines, :]], 1))
        out_ref[lines, :] = (
            jnp.dot(jnp.concatenate([z1, z3, z2], 1), low, preferred_element_type=F32)
            + jnp.dot(z1, w2, preferred_element_type=F32)
            + jnp.dot(z2, w1, preferred_element_type=F32)
        ) + jnp.dot(z1, w1, preferred_element_type=F32)
        copies.append(pltpu.make_async_copy(out_ref.at[lines], out_hbm.at[lines], sem.at[i]))
        copies[-1].start()
    for copy in copies:
        copy.wait()


def body(snapshot, test_matrix):
    dma = pltpu.SemaphoreType.DMA
    hbm = pl.BlockSpec(memory_space=pltpu.HBM)
    vmem = pl.BlockSpec(memory_space=pltpu.VMEM)
    cross, factor, inverse = pl.pallas_call(
        kernel,
        out_shape=(
            jax.ShapeDtypeStruct((2, 2, NY, 256, HALF), F32),
            jax.ShapeDtypeStruct((WIDTH, WIDTH), F32),
            jax.ShapeDtypeStruct((WIDTH, WIDTH), F32),
        ),
        in_specs=[hbm, hbm],
        out_specs=(vmem, vmem, vmem),
        scratch_shapes=[
            pltpu.VMEM((POINTS, SNAPS), F32),
            pltpu.VMEM((SNAPS, WIDTH), F32),
            pltpu.VMEM((SNAPS, POINTS), F32),
            pltpu.VMEM((2, POINTS, HALF), F32),
            pltpu.VMEM((2, POINTS, HALF), F32),
            pltpu.VMEM((2, 3, SHARE, HALF), F32),
            pltpu.VMEM((2, 1024, HALF), F32),
            pltpu.VMEM((2, 1024, HALF), F32),
            pltpu.VMEM((2, 1024, HALF), F32),
            pltpu.VMEM((2, 3, 256, HALF), F32),
            pltpu.VMEM((2, 256, HALF), F32),
            pltpu.VMEM((2, 7, 32, HALF), F32),
            pltpu.VMEM((WIDTH, WIDTH), F32),
            pltpu.VMEM((32, WIDTH), F32),
            pltpu.VMEM((8, 8, HALF), F32),
            pltpu.VMEM((4, 8, HALF), F32),
            pltpu.VMEM((7, 8, HALF), F32),
            pltpu.VMEM((4, 2, 8, 8, HALF), F32),
            dma((2, 8)),
            dma((2, 3)), dma((2, 3)), dma((2, 3)), dma((2, 3)),
            dma((2,)), dma((2,)),
            dma((2, 4, 3)), dma((2, 4, 3)),
            dma((2, 7)), dma((2, 7)), dma((2, 7)), dma((2, 7)),
            dma((2, 4, 3)), dma((2, 4, 3)),
            dma((2, 4)), dma((2, 4)),
            dma, dma,
            dma((3,)), dma((3,)),
            dma((7,)), dma((7,)),
            dma((3,)), dma((3,)),
            dma((7,)), dma((7,)),
            dma, dma,
        ],
        compiler_params=pltpu.CompilerParams(
            collective_id=0, has_side_effects=True, vmem_limit_bytes=48 * 1024 * 1024
        ),
        name="range_finder",
    )(*(pltpu.with_memory_space_constraint(value, pltpu.HBM) for value in (snapshot, test_matrix)))
    return pl.pallas_call(
        finish,
        out_shape=(
            jax.ShapeDtypeStruct((SNAPS, WIDTH), F32),
            jax.ShapeDtypeStruct((WIDTH, WIDTH), F32),
        ),
        in_specs=[vmem, vmem, vmem],
        out_specs=(hbm, hbm),
        scratch_shapes=[
            pltpu.VMEM((SNAPS, WIDTH), F32),
            pltpu.VMEM((WIDTH, WIDTH), F32),
            dma((5,)),
        ],
        compiler_params=pltpu.CompilerParams(vmem_limit_bytes=16 * 1024 * 1024),
        name="final_product",
    )(cross.reshape(2, SNAPS, HALF), inverse, factor)


def solution(mesh):
    return jax.shard_map(
        body,
        mesh=mesh,
        in_specs=(P("rows", "cols"), P("cols", None)),
        out_specs=(P("cols", None), P()),
        check_vma=False,
    )
```
